32 devices in a mesh: dp: 4 (over y, core), tensor: 8 (over z, x).
Axes of the slice: x: 2, y: 2, z: 4, core: 2. Of those that a mesh axis runs over, the one named last changes fastest.
Arguments:
- hidden_in: bfloat16 [3072, 2048], P(('dp', 'tensor')), may hold values from -6 to 6
- norm1_gain: bfloat16 [2048], replicated, may hold values from 0.099609375 to 1.8984375
- norm2_gain: bfloat16 [2048], replicated, may hold values from 0.099609375 to 1.8984375
- w_query: bfloat16 [2048, 2048], P(None, 'tensor'), may hold values from -0.125 to 0.125
- w_keyval: bfloat16 [2048, 256], replicated, may hold values from -0.125 to 0.125
- w_out: bfloat16 [2048, 2048], P('tensor'), may hold values from -0.5 to 0.5
- w_fc: bfloat16 [2048, 8192], P(None, 'tensor'), may hold values from -0.125 to 0.125
- w_proj: bfloat16 [8192, 2048], P('tensor'), may hold values from -0.0625 to 0.0625
- prefix_kv: bfloat16 [4, 4096, 256], P('dp', 'tensor'), may hold values from -320 to 320
- owner_ids: int32 [4], replicated, may hold values from 0 to 3, each once
- segment_ids: int32 [4, 768], P('dp'), may hold values from 0 to 11, never falling along the last dimension, each value on 1 to 192 neighbouring positions
Outputs:
- layer_out: bfloat16 [3072, 2048], P(('dp', 'tensor'))
- attended: bfloat16 [3072, 2048], P(('dp', 'tensor'))
The draws below stay inside these ranges and needn't reach their ends.
Inputs may be any that keep to these rules, and one draw needn't show every extreme that they name: `owner_ids`: each stored prefix is extended by exactly one group. `segment_ids`: within a group the request ids never fall; every one of the 12 requests has 1 to 192 tokens, and at least one has exactly 192.
All inputs are finite; a program needn't handle non-finite values.
Results may differ from the reference program's by a relative error of at most 0.015.
Values may be sent and summed in bfloat16 or wider, within the bound.
A program may use at most 128 MiB of HBM per device.

```python
import math
import jax
import jax.numpy as jnp
import numpy as np
from jax import lax

D = 2048
H = 16
DH = 128
FF = 8192
PREFIX = 4096
REQUESTS = 12
S_ROW = 768
GROUPS = 4
TOKENS = 3072
N_TENSOR = 8


def draw_prefix_kv(key, part):
    first_key = jax.random.fold_in(key, 0)
    shape = (GROUPS, PREFIX, 2 * DH)
    result = jnp.clip(jax.random.normal(first_key, shape, jnp.float32), -4.0, 4.0)
    return result.astype(jnp.bfloat16)


def shard_levels(stream_key, extent, cuts, smallest, largest):
    level, own = 1.0, jax.random.fold_in(stream_key, 6)
    for position, parts in cuts:
        heights = jnp.exp(jax.random.uniform(jax.random.fold_in(own, position), (parts,), jnp.float32, smallest / len(cuts), largest / len(cuts)))
        level = level * jnp.repeat(heights, extent[position] // parts).reshape([-1 if axis == position else 1 for axis in range(len(extent))])
    return level


def length_profile(count, total, most, slope):
    loads = [(1 << 20) // math.isqrt(rank ** slope) + 1 for rank in range(2, count + 1)]
    spare, holding = total - most - (count - 1), [1] * (count - 1)
    while spare > 0:
        movable = [i for i in range(count - 1) if holding[i] < most]
        whole, budget = sum([loads[i] for i in movable]), spare
        for i in movable:
            extra = min(most - holding[i], max(1, budget * loads[i] // whole), spare)
            holding[i] = holding[i] + extra
            spare = spare - extra
    return np.array([most] + holding)


def ragged(own_key, number_of, total, bound, slope):
    if number_of == 2:
        one = jax.random.randint(own_key, (), max(1, total - bound), min(bound, total - 1) + 1)
        return jnp.stack([one, total - one])
    sizes = jnp.asarray(length_profile(number_of, total, bound, slope), jnp.int32)
    pairs = (number_of - 1) // 2
    donor, sink = sizes[1:1 + 2 * pairs:2], sizes[2:2 + 2 * pairs:2]
    margin = jnp.minimum(donor - 1, bound - sink)
    moved = jax.random.randint(jax.random.fold_in(own_key, 1), (pairs,), 0, 1 << 20) % (margin + 1)
    sizes = sizes.at[1:1 + 2 * pairs:2].set(donor - moved).at[2:2 + 2 * pairs:2].set(sink + moved)
    return sizes[jax.random.permutation(jax.random.fold_in(own_key, 2), number_of)]


def noise(rng, shape, scale, limit, shards=(), kind=jnp.bfloat16):
    loudness = shard_levels(rng, shape, shards, -0.22, 0.18) if shards else 1.0
    drawn = jax.random.normal(rng, shape, jnp.float32) * scale * loudness
    return jnp.minimum(jnp.maximum(drawn, -limit), limit).astype(kind)


def setup_inputs(seed: int = 0) -> dict:
    key_of = jax.random.split(jax.random.key(seed), 12)
    hidden_in = noise(key_of[0], (TOKENS, D), 1.0, 6.0, ((0, 32),))
    norm1_gain = jnp.clip(1.0 + 0.18 * jax.random.normal(key_of[1], (D,), jnp.float32), 0.099609375, 1.8984375).astype(jnp.bfloat16)
    norm2_gain = jnp.clip(1.0 + 0.18 * jax.random.normal(key_of[2], (D,), jnp.float32), 0.099609375, 1.8984375).astype(jnp.bfloat16)
    w_query = noise(key_of[3], (D, H * DH), D ** -0.5, 0.125, ((1, 8),))
    w_keyval = noise(key_of[4], (D, 2 * DH), D ** -0.5, 0.125)
    w_out = noise(key_of[5], (H * DH, D), DH ** -0.5, 0.5, ((0, 8),))
    w_fc = noise(key_of[6], (D, FF), D ** -0.5, 0.125, ((1, 8),))
    w_proj = noise(key_of[7], (FF, D), FF ** -0.5, 0.0625, ((0, 8),))
    prefix_kv = draw_prefix_kv(jax.random.fold_in(key_of[11], 71), 0)
    owner_ids = jax.random.permutation(key_of[9], GROUPS).astype(jnp.int32)
    segment_ids = jax.vmap(lambda own: jnp.searchsorted(jnp.cumsum(ragged(own, REQUESTS, S_ROW, S_ROW // 4, 2)), jnp.arange(S_ROW), side="right"))(jax.random.split(key_of[10], GROUPS)).reshape((GROUPS, S_ROW)).astype(jnp.int32)
    return dict(hidden_in=hidden_in, norm1_gain=norm1_gain, norm2_gain=norm2_gain, w_query=w_query, w_keyval=w_keyval, w_out=w_out, w_fc=w_fc, w_proj=w_proj, prefix_kv=prefix_kv, owner_ids=owner_ids, segment_ids=segment_ids)


HIGHEST = lax.Precision.HIGHEST

def layer_norm(values, scales):
    widened = values.astype(jnp.float32)
    centre = lax.optimization_barrier(jnp.mean(widened, axis=-1, keepdims=True))
    centred = widened - centre
    variance = lax.optimization_barrier(jnp.mean(centred * centred, axis=-1, keepdims=True))
    return (centred * lax.rsqrt(variance + 1e-05) * scales.astype(jnp.float32)).astype(jnp.bfloat16)

def reference(hidden_in, norm1_gain, norm2_gain, w_query, w_keyval, w_out, w_fc, w_proj, prefix_kv, owner_ids, segment_ids):
    groups = owner_ids.shape[0]
    row_len = hidden_in.shape[0] // groups
    heads_dev = H // N_TENSOR
    q_scale = 1.0 / math.sqrt(DH)
    inputs = hidden_in.reshape(groups, row_len, D)
    cached_all = jnp.take(prefix_kv, owner_ids.astype(jnp.int32), axis=0)
    positions = jnp.arange(row_len, dtype=jnp.int32)

    def one_row(packed):
        row_rows, cache_rows, request_ids = packed
        normed = layer_norm(row_rows, norm1_gain)
        queries = (jnp.dot(normed, w_query, preferred_element_type=jnp.float32) * q_scale).astype(jnp.bfloat16)
        suffix_kv = jnp.dot(normed, w_keyval, preferred_element_type=jnp.float32).astype(jnp.bfloat16)
        key_rows = jnp.concatenate([cache_rows[:, :DH], suffix_kv[:, :DH]], axis=0).astype(jnp.float32)
        value_rows = jnp.concatenate([cache_rows[:, DH:], suffix_kv[:, DH:]], axis=0)
        suffix_ok = (positions[None, :] <= positions[:, None]) & (request_ids[None, :] == request_ids[:, None])
        allowed = jnp.concatenate([jnp.ones((row_len, PREFIX), dtype=bool), suffix_ok], axis=1)
        head_queries = queries.astype(jnp.float32).reshape(row_len, H, DH).transpose(1, 0, 2)

        def one_head(head_q):
            scores = jnp.dot(head_q, key_rows.T, precision=HIGHEST)
            scores = jnp.where(allowed, scores, -jnp.inf)
            row_top = lax.optimization_barrier(jnp.max(scores, axis=-1, keepdims=True))
            probs = jnp.exp(scores - row_top)
            totals = lax.optimization_barrier(jnp.sum(probs, axis=-1, keepdims=True))
            probs_b = probs.astype(jnp.bfloat16)
            return (jnp.dot(probs_b, value_rows, preferred_element_type=jnp.float32) / totals).astype(jnp.bfloat16)
        attn_heads = lax.map(one_head, head_queries)
        grouped = attn_heads.reshape(N_TENSOR, heads_dev, row_len, DH).transpose(0, 2, 1, 3).reshape(N_TENSOR, row_len, heads_dev * DH)
        out_grouped = w_out.reshape(N_TENSOR, heads_dev * DH, D)
        partials = jnp.einsum('gtc,gcd->gtd', grouped.astype(jnp.float32), out_grouped.astype(jnp.float32), precision=HIGHEST).astype(jnp.bfloat16)
        attended = lax.optimization_barrier(jnp.sum(partials.astype(jnp.float32), axis=0)).astype(jnp.bfloat16)
        middle = (row_rows.astype(jnp.float32) + attended.astype(jnp.float32)).astype(jnp.bfloat16)
        normed2 = layer_norm(middle, norm2_gain)
        hidden_act = jax.nn.gelu(jnp.dot(normed2, w_fc, preferred_element_type=jnp.float32), approximate=True).astype(jnp.bfloat16)
        act_grouped = hidden_act.reshape(row_len, N_TENSOR, FF // N_TENSOR).transpose(1, 0, 2)
        proj_grouped = w_proj.reshape(N_TENSOR, FF // N_TENSOR, D)
        mlp_parts = jnp.einsum('gtf,gfd->gtd', act_grouped.astype(jnp.float32), proj_grouped.astype(jnp.float32), precision=HIGHEST).astype(jnp.bfloat16)
        mlp_sum = lax.optimization_barrier(jnp.sum(mlp_parts.astype(jnp.float32), axis=0))
        layer_out = (middle.astype(jnp.float32) + mlp_sum).astype(jnp.bfloat16)
        return (layer_out, attended)
    outs_rows, attended_rows = lax.map(one_row, (inputs, cached_all, segment_ids))
    return (outs_rows.reshape(groups * row_len, D), attended_rows.reshape(groups * row_len, D))
```

```python
import functools
import math

import jax
import jax.numpy as jnp
from jax import lax
from jax.experimental import pallas as pl
from jax.experimental.pallas import tpu as pltpu
from jax.sharding import PartitionSpec as P

MESH = pl.DeviceIdType.MESH
ROWS = 16


def plane(n):
    lines = 4 if n % 4 == 0 else n
    return lines, n // lines


def norm_rows(widened, gains):
    centre = jnp.mean(widened, axis=-1, keepdims=True)
    centred = widened - centre
    variance = jnp.mean(centred * centred, axis=-1, keepdims=True)
    return (centred * lax.rsqrt(variance + 1e-05) * gains).astype(jnp.bfloat16)


def row_loop(rows, body):
    def step(i, carry):
        body(pl.ds(pl.multiple_of(i * ROWS, ROWS), ROWS))
        return carry

    lax.fori_loop(0, rows // ROWS, step, 0)


class Place:
    def __init__(self, n):
        self.n = n
        self.A, self.B = plane(n)
        self.me = lax.axis_index("tensor")
        self.a = self.me // self.B
        self.b = self.me % self.B

    def across(self, o):
        return (self.b + o) % self.B

    def peer(self, a, b):
        return {"tensor": a * self.B + b}


def greet(place, dp_peers=0):
    barrier = pltpu.get_barrier_semaphore()
    pc = place

    def signal(device):
        pl.semaphore_signal(barrier, inc=1, device_id=device, device_id_type=MESH)

    @pl.when(pc.a > 0)
    def _():
        signal(pc.peer(pc.a - 1, pc.b))

    @pl.when(pc.a < pc.A - 1)
    def _():
        signal(pc.peer(pc.a + 1, pc.b))

    for o in range(1, pc.B):
        signal(pc.peer(pc.a, pc.across(o)))
    dp = lax.axis_index("dp")
    for o in range(1, dp_peers):
        signal({"dp": (dp + o) % dp_peers})
    count = pc.B - 1 + max(dp_peers - 1, 0)
    ends = jnp.where((pc.a == 0) | (pc.a == pc.A - 1), 1, 2)
    pl.semaphore_wait(barrier, count + ends)


def remote(src, dst, send, recv, device):
    return pltpu.make_async_remote_copy(
        src_ref=src, dst_ref=dst, send_sem=send, recv_sem=recv, device_id=device, device_id_type=MESH
    )


class Gather:
    def __init__(self, place, buf, recv, up, down, side):
        self.pc, self.buf, self.recv, self.up, self.down, self.side = place, buf, recv, up, down, side

    def copy_up(self, a0):
        pc = self.pc
        blk = a0 * pc.B + pc.b
        return remote(self.buf.at[blk], self.buf.at[blk], self.up.at[a0], self.recv.at[blk],
                      pc.peer(jnp.minimum(pc.a + 1, pc.A - 1), pc.b))

    def copy_down(self, a0):
        pc = self.pc
        blk = a0 * pc.B + pc.b
        return remote(self.buf.at[blk], self.buf.at[blk], self.down.at[a0], self.recv.at[blk],
                      pc.peer(jnp.maximum(pc.a - 1, 0), pc.b))

    def copy_side(self, a0, o):
        pc = self.pc
        blk = a0 * pc.B + pc.b
        return remote(self.buf.at[blk], self.buf.at[blk], self.side.at[a0, o - 1], self.recv.at[blk],
                      pc.peer(pc.a, pc.across(o)))

    def arrived(self, blk):
        pc = self.pc
        remote(self.buf.at[blk], self.buf.at[blk], self.up.at[0], self.recv.at[blk],
               pc.peer(pc.a, pc.across(1))).wait_recv()

    def start(self):
        pc = self.pc

        @pl.when(pc.a < pc.A - 1)
        def _():
            self.copy_up(pc.a).start()

        @pl.when(pc.a > 0)
        def _():
            self.copy_down(pc.a).start()

        for o in range(1, pc.B):
            self.copy_side(pc.a, o).start()

    def round(self, r, use=None):
        pc = self.pc

        @pl.when(pc.a - r >= 0)
        def _():
            a0 = pc.a - r
            self.arrived(a0 * pc.B + pc.b)

            @pl.when(pc.a < pc.A - 1)
            def _():
                self.copy_up(a0).start()

            for o in range(1, pc.B):
                self.copy_side(a0, o).start()

        @pl.when(pc.a + r < pc.A)
        def _():
            a0 = pc.a + r
            self.arrived(a0 * pc.B + pc.b)

            @pl.when(pc.a > 0)
            def _():
                self.copy_down(a0).start()

            for o in range(1, pc.B):
                self.copy_side(a0, o).start()

    def rounds(self):
        for r in range(1, self.pc.A):
            self.round(r)

    def finish(self):
        pc = self.pc
        for a0 in range(pc.A):
            for o in range(1, pc.B):
                self.arrived(a0 * pc.B + pc.across(o))
        for a0 in range(pc.A):
            for o in range(1, pc.B):
                self.copy_side(a0, o).wait_send()

            @pl.when((pc.a >= a0) & (pc.a < pc.A - 1))
            def _():
                self.copy_up(a0).wait_send()

            @pl.when((pc.a <= a0) & (pc.a > 0))
            def _():
                self.copy_down(a0).wait_send()


def gather_sems(n):
    A, B = plane(n)
    dma = pltpu.SemaphoreType.DMA
    return [dma((n,)), dma((A,)), dma((A,)), dma((A, max(B - 1, 1)))]


class Scatter:
    def __init__(self, place, term, side_in, up_in, down_in, up_out, down_out,
                 side_send, side_recv, up_send, up_recv, down_send, down_recv):
        self.pc, self.term = place, term
        self.side_in, self.up_in, self.down_in = side_in, up_in, down_in
        self.up_out, self.down_out = up_out, down_out
        self.side_send, self.side_recv = side_send, side_recv
        self.up_send, self.up_recv = up_send, up_recv
        self.down_send, self.down_recv = down_send, down_recv
        self.rows = term.shape[1]

    def copy_side(self, a0, o):
        pc = self.pc
        return remote(self.term.at[a0 * pc.B + pc.across(o)], self.side_in.at[a0, o - 1],
                      self.side_send.at[a0, o - 1], self.side_recv.at[a0, o - 1],
                      pc.peer(pc.a, pc.across(o)))

    def copy_up(self, d):
        pc = self.pc
        return remote(self.up_out.at[d], self.up_in.at[d], self.up_send.at[d], self.up_recv.at[d],
                      pc.peer(jnp.minimum(pc.a + 1, pc.A - 1), pc.b))

    def copy_down(self, d):
        pc = self.pc
        return remote(self.down_out.at[d], self.down_in.at[d], self.down_send.at[d], self.down_recv.at[d],
                      pc.peer(jnp.maximum(pc.a - 1, 0), pc.b))

    def start(self):
        pc = self.pc
        for r in range(pc.A - 1, 0, -1):
            for sign in (1, -1):
                d = pc.a + sign * r

                @pl.when((d >= 0) & (d < pc.A))
                def _():
                    for o in range(1, pc.B):
                        self.copy_side(d, o).start()
        for o in range(1, pc.B):
            self.copy_side(pc.a, o).start()

    def local(self, d, rows):
        pc = self.pc
        total = self.term[d * pc.B + pc.b, rows, :].astype(jnp.float32)
        for o in range(1, pc.B):
            total = total + self.side_in[d, o - 1, rows, :].astype(jnp.float32)
        return total

    def forward(self, d, first, arrived, out, make_copy):
        pc = self.pc
        for o in range(1, pc.B):
            self.copy_side(d, o).wait_recv()

        @pl.when(first)
        def _():
            def body(rows):
                out[d, rows, :] = self.local(d, rows).astype(jnp.bfloat16)

            row_loop(self.rows, body)

        @pl.when(jnp.logical_not(first))
        def _():
            make_copy(d).wait_recv()

            def body(rows):
                out[d, rows, :] = (self.local(d, rows) + arrived[d, rows, :].astype(jnp.float32)).astype(jnp.bfloat16)

            row_loop(self.rows, body)

        make_copy(d).start()

    def rounds(self):
        pc = self.pc
        for r in range(pc.A - 1, 0, -1):
            @pl.when(pc.a + r < pc.A)
            def _():
                self.forward(pc.a + r, pc.a == 0, self.up_in, self.up_out, self.copy_up)

            @pl.when(pc.a - r >= 0)
            def _():
                self.forward(pc.a - r, pc.a == pc.A - 1, self.down_in, self.down_out, self.copy_down)

    def result(self, use):
        pc = self.pc
        for o in range(1, pc.B):
            self.copy_side(pc.a, o).wait_recv()

        @pl.when(pc.a == 0)
        def _():
            self.copy_down(pc.a).wait_recv()
            row_loop(self.rows, lambda rows: use(
                rows, self.local(pc.a, rows) + self.down_in[pc.a, rows, :].astype(jnp.float32)))

        @pl.when(pc.a == pc.A - 1)
        def _():
            self.copy_up(pc.a).wait_recv()
            row_loop(self.rows, lambda rows: use(
                rows, self.local(pc.a, rows) + self.up_in[pc.a, rows, :].astype(jnp.float32)))

        @pl.when((pc.a > 0) & (pc.a < pc.A - 1))
        def _():
            self.copy_up(pc.a).wait_recv()
            self.copy_down(pc.a).wait_recv()
            row_loop(self.rows, lambda rows: use(
                rows, self.local(pc.a, rows) + self.up_in[pc.a, rows, :].astype(jnp.float32)
                + self.down_in[pc.a, rows, :].astype(jnp.float32)))

    def finish(self):
        pc = self.pc
        for d in range(pc.A):
            for o in range(1, pc.B):
                self.copy_side(d, o).wait_send()

            @pl.when(pc.a < d)
            def _():
                self.copy_up(d).wait_send()

            @pl.when(pc.a > d)
            def _():
                self.copy_down(d).wait_send()


def scatter_scratch(n, rows, width):
    A, B = plane(n)
    dma = pltpu.SemaphoreType.DMA
    side = max(B - 1, 1)
    buf = pltpu.VMEM((A, rows, width), jnp.bfloat16)
    return [pltpu.VMEM((A, side, rows, width), jnp.bfloat16), buf, buf, buf, buf,
            dma((A, side)), dma((A, side)), dma((A,)), dma((A,)), dma((A,)), dma((A,))]


def enter_kernel(n, ndp, hidden, gain, prefix, owners, normed, cached,
                 from_dp, dp_send, dp_recv, *sems):
    pc = Place(n)
    dp = lax.axis_index("dp")
    greet(pc, ndp)

    def to_dp(o):
        return remote(prefix.at[0], from_dp.at[dp], dp_send.at[o - 1], dp_recv.at[dp],
                      {"dp": (dp + o) % ndp})

    for o in range(1, ndp):
        to_dp(o).start()
    gains = gain[...].astype(jnp.float32)

    def first(rows):
        normed[pc.me, rows, :] = norm_rows(hidden[rows, :].astype(jnp.float32), gains)

    row_loop(hidden.shape[0], first)
    tokens = Gather(pc, normed, *sems[:4])
    tokens.start()
    from_dp[dp] = prefix[0]
    tokens.rounds()
    for o in range(1, ndp):
        src = (dp + o) % ndp
        remote(prefix.at[0], from_dp.at[src], dp_send.at[0], dp_recv.at[src],
               {"dp": (dp + 1) % ndp}).wait_recv()
    cached[pc.me] = from_dp[owners[dp]]
    keys = Gather(pc, cached, *sems[4:])
    keys.start()
    keys.rounds()
    tokens.finish()
    keys.finish()
    for o in range(1, ndp):
        to_dp(o).wait_send()


def middle_kernel(n, term, hidden, gain, attended, middle, normed, *scratch):
    pc = Place(n)
    greet(pc)
    scatter = Scatter(pc, term, *scratch[:11])
    scatter.start()
    scatter.rounds()
    gains = gain[...].astype(jnp.float32)

    def use(rows, total):
        out = total.astype(jnp.bfloat16)
        attended[rows, :] = out
        mid = (hidden[rows, :].astype(jnp.float32) + out.astype(jnp.float32)).astype(jnp.bfloat16)
        middle[rows, :] = mid
        normed[pc.me, rows, :] = norm_rows(mid.astype(jnp.float32), gains)

    scatter.result(use)
    gather = Gather(pc, normed, *scratch[11:])
    gather.start()
    gather.rounds()
    scatter.finish()
    gather.finish()


def leave_kernel(n, term, middle, out, *scratch):
    pc = Place(n)
    greet(pc)
    scatter = Scatter(pc, term, *scratch)
    scatter.start()
    scatter.rounds()

    def use(rows, total):
        out[rows, :] = (middle[rows, :].astype(jnp.float32) + total).astype(jnp.bfloat16)

    scatter.result(use)
    scatter.finish()


VM = pl.BlockSpec(memory_space=pltpu.VMEM)


def params(cid):
    return pltpu.CompilerParams(collective_id=cid, has_side_effects=True, vmem_limit_bytes=48 << 20)


def attend_block(state_in, queries, key_rows, value_rows, allowed):
    running, totals, weighted = state_in
    scores = jnp.einsum("htd,kd->htk", queries, key_rows, preferred_element_type=jnp.float32)
    if allowed is not None:
        scores = jnp.where(allowed[None], scores, -jnp.inf)
    new_top = jnp.maximum(running, jnp.max(scores, axis=-1))
    factor = jnp.exp(running - new_top)
    probs = jnp.exp(scores - new_top[..., None])
    totals = totals * factor + jnp.sum(probs, axis=-1)
    probs_b = probs.astype(jnp.bfloat16)
    weighted = weighted * factor[..., None] + jnp.einsum(
        "htk,kd->htd", probs_b, value_rows, preferred_element_type=jnp.float32
    )
    return (new_top, totals, weighted)


def local(n, ndp, hidden_in, norm1_gain, norm2_gain, w_query, w_keyval, w_out, w_fc, w_proj,
          prefix_kv, owner_ids, segment_ids):
    rows, width = hidden_in.shape
    head_size = w_keyval.shape[1] // 2
    query_cols = w_query.shape[1]
    heads_here = query_cols // head_size
    row_len = segment_ids.shape[1]
    span = prefix_kv.shape[1]
    q_scale = 1.0 / math.sqrt(head_size)
    bf = jnp.bfloat16
    dma = pltpu.SemaphoreType.DMA
    normed, cached = pl.pallas_call(
        functools.partial(enter_kernel, n, ndp),
        out_shape=(jax.ShapeDtypeStruct((n, rows, width), bf),
                   jax.ShapeDtypeStruct((n, span, 2 * head_size), bf)),
        in_specs=[VM, VM, VM, pl.BlockSpec(memory_space=pltpu.SMEM)],
        out_specs=(VM, VM),
        scratch_shapes=[pltpu.VMEM((ndp, span, 2 * head_size), bf), dma((ndp,)), dma((ndp,))]
        + gather_sems(n) + gather_sems(n),
        compiler_params=params(1),
        name="enter",
    )(hidden_in, norm1_gain.reshape(1, -1), prefix_kv, owner_ids)
    normed = normed.reshape(row_len, width)
    fragment = cached.reshape(n * span, 2 * head_size)
    w_joint = jnp.concatenate([w_query, w_keyval], axis=1)
    col_scale = jnp.concatenate(
        [jnp.full((query_cols,), q_scale, jnp.float32), jnp.ones((2 * head_size,), jnp.float32)]
    )
    projected = (jnp.dot(normed, w_joint, preferred_element_type=jnp.float32) * col_scale).astype(bf)
    queries = projected[:, :query_cols].reshape(row_len, heads_here, head_size).transpose(1, 0, 2)
    suffix_keys = projected[:, query_cols : query_cols + head_size]
    suffix_values = projected[:, query_cols + head_size :]
    request_ids = segment_ids[0]
    positions = jnp.arange(row_len, dtype=jnp.int32)
    allowed = (positions[None, :] <= positions[:, None]) & (
        request_ids[None, :] == request_ids[:, None]
    )
    state = (
        jnp.full((heads_here, row_len), -jnp.inf, jnp.float32),
        jnp.zeros((heads_here, row_len), jnp.float32),
        jnp.zeros((heads_here, row_len, head_size), jnp.float32),
    )
    state = attend_block(state, queries, suffix_keys, suffix_values, allowed)
    for row_begin in range(0, fragment.shape[0], 1024):
        block_rows = fragment[row_begin : row_begin + 1024]
        state = attend_block(state, queries, block_rows[:, :head_size], block_rows[:, head_size:], None)
    running, totals, weighted = state
    attn_heads = (
        (weighted / totals[..., None]).astype(bf).transpose(1, 0, 2).reshape(row_len, query_cols)
    )
    term = jnp.dot(attn_heads, w_out, preferred_element_type=jnp.float32).astype(bf)
    own = jax.ShapeDtypeStruct((rows, width), bf)
    attended, middle, normed2 = pl.pallas_call(
        functools.partial(middle_kernel, n),
        out_shape=(own, own, jax.ShapeDtypeStruct((n, rows, width), bf)),
        in_specs=[VM] * 3,
        out_specs=(VM, VM, VM),
        scratch_shapes=scatter_scratch(n, rows, width) + gather_sems(n),
        compiler_params=params(2),
        name="middle",
    )(term.reshape(n, rows, width), hidden_in, norm2_gain.reshape(1, -1))
    hidden_act = jax.nn.gelu(
        jnp.dot(normed2.reshape(row_len, width), w_fc, preferred_element_type=jnp.float32),
        approximate=True,
    ).astype(bf)
    term = jnp.dot(hidden_act, w_proj, preferred_element_type=jnp.float32).astype(bf)
    layer_out = pl.pallas_call(
        functools.partial(leave_kernel, n),
        out_shape=own,
        in_specs=[VM] * 2,
        out_specs=VM,
        scratch_shapes=scatter_scratch(n, rows, width),
        compiler_params=params(3),
        name="leave",
    )(term.reshape(n, rows, width), middle)
    return (layer_out, attended)


def solution(mesh):
    return jax.shard_map(
        functools.partial(local, mesh.shape["tensor"], mesh.shape["dp"]),
        mesh=mesh,
        in_specs=(
            P(("dp", "tensor"), None),
            P(),
            P(),
            P(None, "tensor"),
            P(),
            P("tensor", None),
            P(None, "tensor"),
            P("tensor", None),
            P("dp", "tensor", None),
            P(),
            P("dp", None),
        ),
        out_specs=(P(("dp", "tensor"), None), P(("dp", "tensor"), None)),
        check_vma=False,
    )
```

```python
import functools
import math

import jax
import jax.numpy as jnp
from jax import lax
from jax.experimental import pallas as pl
from jax.experimental.pallas import tpu as pltpu
from jax.sharding import PartitionSpec as P

MESH = pl.DeviceIdType.MESH
ROWS = 16


def plane(n):
    lines = 4 if n % 4 == 0 else n
    return lines, n // lines


def norm_rows(widened, gains):
    centre = jnp.mean(widened, axis=-1, keepdims=True)
    centred = widened - centre
    variance = jnp.mean(centred * centred, axis=-1, keepdims=True)
    return (centred * lax.rsqrt(variance + 1e-05) * gains).astype(jnp.bfloat16)


def row_loop(rows, body):
    def step(i, carry):
        body(pl.ds(pl.multiple_of(i * ROWS, ROWS), ROWS))
        return carry

    lax.fori_loop(0, rows // ROWS, step, 0)


class Place:
    def __init__(self, n):
        self.n = n
        self.A, self.B = plane(n)
        self.me = lax.axis_index("tensor")
        self.a = self.me // self.B
        self.b = self.me % self.B

    def across(self, o):
        return (self.b + o) % self.B

    def peer(self, a, b):
        return {"tensor": a * self.B + b}

    def far(self, k):
        found = 0
        for a in range(self.A):
            order = sorted(range(self.A), key=lambda d: (-abs(d - a), -d))
            for i, d in enumerate(order):
                found = found + jnp.where((self.a == a) & (k == i), d, 0)
        return found


def greet(place, dp_peers=0):
    barrier = pltpu.get_barrier_semaphore()
    pc = place

    def signal(device):
        pl.semaphore_signal(barrier, inc=1, device_id=device, device_id_type=MESH)

    @pl.when(pc.a > 0)
    def _():
        signal(pc.peer(pc.a - 1, pc.b))

    @pl.when(pc.a < pc.A - 1)
    def _():
        signal(pc.peer(pc.a + 1, pc.b))

    for o in range(1, pc.B):
        signal(pc.peer(pc.a, pc.across(o)))
    dp = lax.axis_index("dp")
    for o in range(1, dp_peers):
        signal({"dp": (dp + o) % dp_peers})
    count = pc.B - 1 + max(dp_peers - 1, 0)
    ends = jnp.where((pc.a == 0) | (pc.a == pc.A - 1), 1, 2)
    pl.semaphore_wait(barrier, count + ends)


def remote(src, dst, send, recv, device):
    return pltpu.make_async_remote_copy(
        src_ref=src, dst_ref=dst, send_sem=send, recv_sem=recv, device_id=device, device_id_type=MESH
    )


class Gather:
    def __init__(self, place, buf, recv, up, down, side):
        self.pc, self.buf, self.recv, self.up, self.down, self.side = place, buf, recv, up, down, side

    def copy_up(self, a0):
        pc = self.pc
        blk = a0 * pc.B + pc.b
        return remote(self.buf.at[blk], self.buf.at[blk], self.up.at[a0], self.recv.at[blk],
                      pc.peer(jnp.minimum(pc.a + 1, pc.A - 1), pc.b))

    def copy_down(self, a0):
        pc = self.pc
        blk = a0 * pc.B + pc.b
        return remote(self.buf.at[blk], self.buf.at[blk], self.down.at[a0], self.recv.at[blk],
                      pc.peer(jnp.maximum(pc.a - 1, 0), pc.b))

    def copy_side(self, a0, o):
        pc = self.pc
        blk = a0 * pc.B + pc.b
        return remote(self.buf.at[blk], self.buf.at[blk], self.side.at[a0, o - 1], self.recv.at[blk],
                      pc.peer(pc.a, pc.across(o)))

    def arrived(self, blk):
        pc = self.pc
        remote(self.buf.at[blk], self.buf.at[blk], self.up.at[0], self.recv.at[blk],
               pc.peer(pc.a, pc.across(1))).wait_recv()

    def start(self):
        pc = self.pc

        @pl.when(pc.a < pc.A - 1)
        def _():
            self.copy_up(pc.a).start()

        @pl.when(pc.a > 0)
        def _():
            self.copy_down(pc.a).start()

        for o in range(1, pc.B):
            self.copy_side(pc.a, o).start()

    def round(self, r, use=None):
        pc = self.pc

        @pl.when(pc.a - r >= 0)
        def _():
            a0 = pc.a - r
            self.arrived(a0 * pc.B + pc.b)

            @pl.when(pc.a < pc.A - 1)
            def _():
                self.copy_up(a0).start()

            for o in range(1, pc.B):
                self.copy_side(a0, o).start()

        @pl.when(pc.a + r < pc.A)
        def _():
            a0 = pc.a + r
            self.arrived(a0 * pc.B + pc.b)

            @pl.when(pc.a > 0)
            def _():
                self.copy_down(a0).start()

            for o in range(1, pc.B):
                self.copy_side(a0, o).start()

    def rounds(self):
        for r in range(1, self.pc.A):
            self.round(r)

    def pair_arrived(self, a0):
        for o in range(1, self.pc.B):
            self.arrived(a0 * self.pc.B + self.pc.across(o))

    def finish(self):
        pc = self.pc
        for a0 in range(pc.A):
            for o in range(1, pc.B):
                self.copy_side(a0, o).wait_send()

            @pl.when((pc.a >= a0) & (pc.a < pc.A - 1))
            def _():
                self.copy_up(a0).wait_send()

            @pl.when((pc.a <= a0) & (pc.a > 0))
            def _():
                self.copy_down(a0).wait_send()


def gather_sems(n):
    A, B = plane(n)
    dma = pltpu.SemaphoreType.DMA
    return [dma((n,)), dma((A,)), dma((A,)), dma((A, max(B - 1, 1)))]


class Scatter:
    def __init__(self, place, term, side_in, up_in, down_in, up_out, down_out,
                 side_send, side_recv, up_send, up_recv, down_send, down_recv):
        self.pc, self.term = place, term
        self.side_in, self.up_in, self.down_in = side_in, up_in, down_in
        self.up_out, self.down_out = up_out, down_out
        self.side_send, self.side_recv = side_send, side_recv
        self.up_send, self.up_recv = up_send, up_recv
        self.down_send, self.down_recv = down_send, down_recv
        self.rows = term.shape[1]

    def copy_side(self, a0, o):
        pc = self.pc
        return remote(self.term.at[a0 * pc.B + pc.across(o)], self.side_in.at[a0, o - 1],
                      self.side_send.at[a0, o - 1], self.side_recv.at[a0, o - 1],
                      pc.peer(pc.a, pc.across(o)))

    def copy_up(self, d):
        pc = self.pc
        return remote(self.up_out.at[d], self.up_in.at[d], self.up_send.at[d], self.up_recv.at[d],
                      pc.peer(jnp.minimum(pc.a + 1, pc.A - 1), pc.b))

    def copy_down(self, d):
        pc = self.pc
        return remote(self.down_out.at[d], self.down_in.at[d], self.down_send.at[d], self.down_recv.at[d],
                      pc.peer(jnp.maximum(pc.a - 1, 0), pc.b))

    def start(self, d):
        for o in range(1, self.pc.B):
            self.copy_side(d, o).start()

    def local(self, d, rows):
        pc = self.pc
        total = self.term[d * pc.B + pc.b, rows, :].astype(jnp.float32)
        for o in range(1, pc.B):
            total = total + self.side_in[d, o - 1, rows, :].astype(jnp.float32)
        return total

    def forward(self, d, first, arrived, out, make_copy):
        pc = self.pc
        for o in range(1, pc.B):
            self.copy_side(d, o).wait_recv()

        @pl.when(first)
        def _():
            def body(rows):
                out[d, rows, :] = self.local(d, rows).astype(jnp.bfloat16)

            row_loop(self.rows, body)

        @pl.when(jnp.logical_not(first))
        def _():
            make_copy(d).wait_recv()

            def body(rows):
                out[d, rows, :] = (self.local(d, rows) + arrived[d, rows, :].astype(jnp.float32)).astype(jnp.bfloat16)

            row_loop(self.rows, body)

        make_copy(d).start()

    def pass_on(self, d):
        pc = self.pc

        @pl.when(d > pc.a)
        def _():
            self.forward(d, pc.a == 0, self.up_in, self.up_out, self.copy_up)

        @pl.when(d < pc.a)
        def _():
            self.forward(d, pc.a == pc.A - 1, self.down_in, self.down_out, self.copy_down)

    def run(self, compute):
        pc = self.pc
        end = (pc.a == 0) | (pc.a == pc.A - 1)

        def step(k, carry):
            d = pc.far(k)
            compute(d)
            self.start(d)

            @pl.when((k >= 1) & end)
            def _():
                self.pass_on(pc.far(k - 1))

            return carry

        lax.fori_loop(0, pc.A, step, 0)

        @pl.when(jnp.logical_not(end))
        def _():
            def late(k, carry):
                self.pass_on(pc.far(k))
                return carry

            lax.fori_loop(0, pc.A - 1, late, 0)

    def result(self, use):
        pc = self.pc
        for o in range(1, pc.B):
            self.copy_side(pc.a, o).wait_recv()

        @pl.when(pc.a == 0)
        def _():
            self.copy_down(pc.a).wait_recv()
            row_loop(self.rows, lambda rows: use(
                rows, self.local(pc.a, rows) + self.down_in[pc.a, rows, :].astype(jnp.float32)))

        @pl.when(pc.a == pc.A - 1)
        def _():
            self.copy_up(pc.a).wait_recv()
            row_loop(self.rows, lambda rows: use(
                rows, self.local(pc.a, rows) + self.up_in[pc.a, rows, :].astype(jnp.float32)))

        @pl.when((pc.a > 0) & (pc.a < pc.A - 1))
        def _():
            self.copy_up(pc.a).wait_recv()
            self.copy_down(pc.a).wait_recv()
            row_loop(self.rows, lambda rows: use(
                rows, self.local(pc.a, rows) + self.up_in[pc.a, rows, :].astype(jnp.float32)
                + self.down_in[pc.a, rows, :].astype(jnp.float32)))

    def finish(self):
        pc = self.pc
        for d in range(pc.A):
            for o in range(1, pc.B):
                self.copy_side(d, o).wait_send()

            @pl.when(pc.a < d)
            def _():
                self.copy_up(d).wait_send()

            @pl.when(pc.a > d)
            def _():
                self.copy_down(d).wait_send()


def scatter_scratch(n, rows, width):
    A, B = plane(n)
    dma = pltpu.SemaphoreType.DMA
    side = max(B - 1, 1)
    buf = pltpu.VMEM((A, rows, width), jnp.bfloat16)
    return [pltpu.VMEM((A, side, rows, width), jnp.bfloat16), buf, buf, buf, buf,
            dma((A, side)), dma((A, side)), dma((A,)), dma((A,)), dma((A,)), dma((A,))]


def enter_kernel(n, ndp, q_scale, hidden, gain, prefix, w_query, w_keyval, owners, projected, cached,
                 normed, from_dp, dp_send, dp_recv, *sems):
    pc = Place(n)
    dp = lax.axis_index("dp")
    greet(pc, ndp)
    rows, width = hidden.shape
    slab = pc.B * rows
    query_cols = w_query.shape[1]

    def to_dp(o):
        return remote(prefix.at[0], from_dp.at[dp], dp_send.at[o - 1], dp_recv.at[dp],
                      {"dp": (dp + o) % ndp})

    gains = gain[...].astype(jnp.float32)

    def first(part):
        normed[pc.me, part, :] = norm_rows(hidden[part, :].astype(jnp.float32), gains)

    row_loop(rows, first)
    tokens = Gather(pc, normed, *sems[:4])
    tokens.start()
    for o in range(1, ndp):
        to_dp(o).start()
    from_dp[dp] = prefix[0]

    def project(d):
        tokens.pair_arrived(d)
        left = normed[pl.ds(d * pc.B, pc.B)].reshape(slab, width)
        here = pl.ds(pl.multiple_of(d * slab, slab), slab)
        projected[here, :query_cols] = (
            jnp.dot(left, w_query[...], preferred_element_type=jnp.float32) * q_scale
        ).astype(jnp.bfloat16)
        projected[here, query_cols:] = jnp.dot(
            left, w_keyval[...], preferred_element_type=jnp.float32
        ).astype(jnp.bfloat16)

    for r in range(1, pc.A):
        tokens.round(r)
        if r < pc.A - 1:
            project(pc.far(pc.A - r))
    for o in range(1, ndp):
        src = (dp + o) % ndp
        remote(prefix.at[0], from_dp.at[src], dp_send.at[0], dp_recv.at[src],
               {"dp": (dp + 1) % ndp}).wait_recv()
    cached[pc.me] = from_dp[owners[dp]]
    keys = Gather(pc, cached, *sems[4:])
    keys.start()
    project(pc.far(1))
    keys.round(1)
    project(pc.far(0))
    for r in range(2, pc.A):
        keys.round(r)
    for a0 in range(pc.A):
        keys.pair_arrived(a0)
    tokens.finish()
    keys.finish()
    for o in range(1, ndp):
        to_dp(o).wait_send()


def core_kernel(n, heads, projected, cached, seg_rows, seg_cols, w_out, hidden, gain, w_fc_hbm, w_proj_hbm,
                attended, layer_out, *scratch):
    pc = Place(n)
    w_fc, w_proj, fc_sem, proj_sem, term, term2, normed, middle, act = scratch[:9]
    greet(pc)
    load_fc = pltpu.make_async_copy(w_fc_hbm, w_fc, fc_sem)
    load_proj = pltpu.make_async_copy(w_proj_hbm, w_proj, proj_sem)
    load_fc.start()
    load_proj.start()
    rows, width = hidden.shape
    slab = pc.B * rows
    row_len = projected.shape[0]
    head = cached.shape[1] // 2
    q_cols = heads * head
    span = min(1024, cached.shape[0])

    def block(q, state, keys, values, allowed):
        top, total, weighted = state
        scores = lax.dot_general(q, keys, (((1,), (1,)), ((), ())), preferred_element_type=jnp.float32)
        if allowed is not None:
            scores = jnp.where(allowed[None], scores.reshape(heads, slab, -1), -jnp.inf)
            scores = scores.reshape(heads * slab, -1)
        new_top = jnp.maximum(top, jnp.max(scores, axis=-1, keepdims=True))
        factor = jnp.exp(top - new_top)
        probs = jnp.exp(scores - new_top)
        total = total * factor + jnp.sum(probs, axis=-1, keepdims=True)
        weighted = weighted * factor + jnp.dot(
            probs.astype(jnp.bfloat16), values, preferred_element_type=jnp.float32
        )
        return new_top, total, weighted

    def emit(left, weights, cols, target, d):
        wide = min(512, width)

        def column(c, carry):
            here = pl.ds(pl.multiple_of(c * wide, wide), wide)
            out = jnp.dot(left, weights[:, here], preferred_element_type=jnp.float32)
            target[pl.ds(d * pc.B, pc.B), :, here] = out.astype(jnp.bfloat16).reshape(pc.B, rows, wide)
            return carry

        lax.fori_loop(0, width // wide, column, 0)

    def attend(d):
        here = pl.ds(pl.multiple_of(d * slab, slab), slab)
        q = jnp.concatenate([projected[here, h * head : (h + 1) * head] for h in range(heads)], axis=0)
        state = (
            jnp.full((heads * slab, 1), -jnp.inf, jnp.float32),
            jnp.zeros((heads * slab, 1), jnp.float32),
            jnp.zeros((heads * slab, head), jnp.float32),
        )

        def over(i, state):
            part = pl.ds(pl.multiple_of(i * span, span), span)
            return block(q, state, cached[part, :head], cached[part, head:], None)

        state = lax.fori_loop(0, cached.shape[0] // span, over, state)
        place = d * slab + lax.broadcasted_iota(jnp.int32, (slab, row_len), 0)
        other = lax.broadcasted_iota(jnp.int32, (slab, row_len), 1)
        allowed = (other <= place) & (seg_rows[here, :] == seg_cols[...])
        top, total, weighted = block(
            q, state, projected[:, q_cols : q_cols + head], projected[:, q_cols + head :], allowed
        )
        out = (weighted / total).astype(jnp.bfloat16)
        left = jnp.concatenate([out[h * slab : (h + 1) * slab] for h in range(heads)], axis=1)
        emit(left, w_out, q_cols, term, d)

    scatter = Scatter(pc, term, *scratch[9:20])
    scatter.run(attend)
    gains = gain[...].astype(jnp.float32)

    def use(part, total):
        out = total.astype(jnp.bfloat16)
        attended[part, :] = out
        mid = (hidden[part, :].astype(jnp.float32) + out.astype(jnp.float32)).astype(jnp.bfloat16)
        middle[part, :] = mid
        normed[pc.me, part, :] = norm_rows(mid.astype(jnp.float32), gains)

    scatter.result(use)
    gather = Gather(pc, normed, *scratch[20:24])
    gather.start()
    load_fc.wait()
    load_proj.wait()
    units = w_fc.shape[1]
    wide = min(256, units)

    def expand(d):
        gather.pair_arrived(d)
        here = pl.ds(pl.multiple_of(d * slab, slab), slab)

        def column(c, carry):
            cols = pl.ds(pl.multiple_of(c * wide, wide), wide)
            left = normed[pl.ds(d * pc.B, pc.B)].reshape(slab, width)
            out = jnp.dot(left, w_fc[:, cols], preferred_element_type=jnp.float32)
            act[here, cols] = jax.nn.gelu(out, approximate=True).astype(jnp.bfloat16)
            return carry

        lax.fori_loop(0, units // wide, column, 0)

    for r in range(1, pc.A):
        gather.round(r)
        expand(pc.far(pc.A - r))
    expand(pc.far(0))

    def contract(d):
        here = pl.ds(pl.multiple_of(d * slab, slab), slab)
        emit(act[here, :], w_proj, units, term2, d)

    scatter2 = Scatter(pc, term2, *scratch[24:])
    scatter2.run(contract)

    def last(part, total):
        layer_out[part, :] = (middle[part, :].astype(jnp.float32) + total).astype(jnp.bfloat16)

    scatter2.result(last)
    scatter.finish()
    gather.finish()
    scatter2.finish()


VM = pl.BlockSpec(memory_space=pltpu.VMEM)


def params(cid):
    return pltpu.CompilerParams(collective_id=cid, has_side_effects=True, vmem_limit_bytes=60 << 20)


def local(n, ndp, hidden_in, norm1_gain, norm2_gain, w_query, w_keyval, w_out, w_fc, w_proj,
          prefix_kv, owner_ids, segment_ids):
    rows, width = hidden_in.shape
    head_size = w_keyval.shape[1] // 2
    query_cols = w_query.shape[1]
    heads_here = query_cols // head_size
    row_len = segment_ids.shape[1]
    span = prefix_kv.shape[1]
    q_scale = 1.0 / math.sqrt(head_size)
    bf = jnp.bfloat16
    dma = pltpu.SemaphoreType.DMA
    any_space = pl.BlockSpec(memory_space=pl.ANY)
    projected, cached = pl.pallas_call(
        functools.partial(enter_kernel, n, ndp, q_scale),
        out_shape=(jax.ShapeDtypeStruct((row_len, query_cols + 2 * head_size), bf),
                   jax.ShapeDtypeStruct((n, span, 2 * head_size), bf)),
        in_specs=[VM] * 5 + [pl.BlockSpec(memory_space=pltpu.SMEM)],
        out_specs=(VM, VM),
        scratch_shapes=[pltpu.VMEM((n, rows, width), bf), pltpu.VMEM((ndp, span, 2 * head_size), bf),
                        dma((ndp,)), dma((ndp,))] + gather_sems(n) + gather_sems(n),
        compiler_params=params(1),
        name="enter",
    )(hidden_in, norm1_gain.reshape(1, -1), prefix_kv, w_query, w_keyval, owner_ids)
    own = jax.ShapeDtypeStruct((rows, width), bf)
    terms = pltpu.VMEM((n, rows, width), bf)
    attended, layer_out = pl.pallas_call(
        functools.partial(core_kernel, n, heads_here),
        out_shape=(own, own),
        in_specs=[VM] * 7 + [any_space] * 2,
        out_specs=(VM, VM),
        scratch_shapes=[pltpu.VMEM(w_fc.shape, bf), pltpu.VMEM(w_proj.shape, bf), dma(()), dma(()),
                        terms, terms, terms, pltpu.VMEM((rows, width), bf),
                        pltpu.VMEM((row_len, w_fc.shape[1]), bf)]
        + scatter_scratch(n, rows, width) + gather_sems(n) + scatter_scratch(n, rows, width),
        compiler_params=params(2),
        name="core",
    )(projected, cached.reshape(n * span, 2 * head_size), segment_ids.reshape(-1, 1),
      segment_ids.reshape(1, -1), w_out, hidden_in, norm2_gain.reshape(1, -1), w_fc, w_proj)
    return (layer_out, attended)


def solution(mesh):
    return jax.shard_map(
        functools.partial(local, mesh.shape["tensor"], mesh.shape["dp"]),
        mesh=mesh,
        in_specs=(
            P(("dp", "tensor"), None),
            P(),
            P(),
            P(None, "tensor"),
            P(),
            P("tensor", None),
            P(None, "tensor"),
            P("tensor", None),
            P("dp", "tensor", None),
            P(),
            P("dp", None),
        ),
        out_specs=(P(("dp", "tensor"), None), P(("dp", "tensor"), None)),
        check_vma=False,
    )
```

```python
import functools
import math

import jax
import jax.numpy as jnp
from jax import lax
from jax.experimental import pallas as pl
from jax.experimental.pallas import tpu as pltpu
from jax.sharding import PartitionSpec as P

MESH = pl.DeviceIdType.MESH
ROWS = 16


def plane(n):
    lines = 4 if n % 4 == 0 else n
    return lines, n // lines


def norm_rows(widened, gains):
    centre = jnp.mean(widened, axis=-1, keepdims=True)
    centred = widened - centre
    variance = jnp.mean(centred * centred, axis=-1, keepdims=True)
    return (centred * lax.rsqrt(variance + 1e-05) * gains).astype(jnp.bfloat16)


def row_loop(rows, body):
    def step(i, carry):
        body(pl.ds(pl.multiple_of(i * ROWS, ROWS), ROWS))
        return carry

    lax.fori_loop(0, rows // ROWS, step, 0)


class Place:
    def __init__(self, n):
        self.n = n
        self.A, self.B = plane(n)
        self.me = lax.axis_index("tensor")
        self.a = self.me // self.B
        self.b = self.me % self.B

    def across(self, o):
        return (self.b + o) % self.B

    def peer(self, a, b):
        return {"tensor": a * self.B + b}

    def far(self, k):
        found = 0
        for a in range(self.A):
            order = sorted(range(self.A), key=lambda d: (-abs(d - a), -d))
            for i, d in enumerate(order):
                found = found + jnp.where((self.a == a) & (k == i), d, 0)
        return found


def greet(place, dp_peers=0):
    barrier = pltpu.get_barrier_semaphore()
    pc = place

    def signal(device):
        pl.semaphore_signal(barrier, inc=1, device_id=device, device_id_type=MESH)

    @pl.when(pc.a > 0)
    def _():
        signal(pc.peer(pc.a - 1, pc.b))

    @pl.when(pc.a < pc.A - 1)
    def _():
        signal(pc.peer(pc.a + 1, pc.b))

    for o in range(1, pc.B):
        signal(pc.peer(pc.a, pc.across(o)))
    dp = lax.axis_index("dp")
    for o in range(1, dp_peers):
        signal({"dp": (dp + o) % dp_peers})
    count = pc.B - 1 + max(dp_peers - 1, 0)
    ends = jnp.where((pc.a == 0) | (pc.a == pc.A - 1), 1, 2)
    pl.semaphore_wait(barrier, count + ends)


def remote(src, dst, send, recv, device):
    return pltpu.make_async_remote_copy(
        src_ref=src, dst_ref=dst, send_sem=send, recv_sem=recv, device_id=device, device_id_type=MESH
    )


class Gather:
    def __init__(self, place, buf, recv, up, down, side):
        self.pc, self.buf, self.recv, self.up, self.down, self.side = place, buf, recv, up, down, side

    def copy_up(self, a0):
        pc = self.pc
        blk = a0 * pc.B + pc.b
        return remote(self.buf.at[blk], self.buf.at[blk], self.up.at[a0], self.recv.at[blk],
                      pc.peer(jnp.minimum(pc.a + 1, pc.A - 1), pc.b))

    def copy_down(self, a0):
        pc = self.pc
        blk = a0 * pc.B + pc.b
        return remote(self.buf.at[blk], self.buf.at[blk], self.down.at[a0], self.recv.at[blk],
                      pc.peer(jnp.maximum(pc.a - 1, 0), pc.b))

    def copy_side(self, a0, o):
        pc = self.pc
        blk = a0 * pc.B + pc.b
        return remote(self.buf.at[blk], self.buf.at[blk], self.side.at[a0, o - 1], self.recv.at[blk],
                      pc.peer(pc.a, pc.across(o)))

    def arrived(self, blk):
        pc = self.pc
        remote(self.buf.at[blk], self.buf.at[blk], self.up.at[0], self.recv.at[blk],
               pc.peer(pc.a, pc.across(1))).wait_recv()

    def start(self):
        pc = self.pc

        @pl.when(pc.a < pc.A - 1)
        def _():
            self.copy_up(pc.a).start()

        @pl.when(pc.a > 0)
        def _():
            self.copy_down(pc.a).start()

        for o in range(1, pc.B):
            self.copy_side(pc.a, o).start()

    def round(self, r, use=None):
        pc = self.pc

        @pl.when(pc.a - r >= 0)
        def _():
            a0 = pc.a - r
            self.arrived(a0 * pc.B + pc.b)

            @pl.when(pc.a < pc.A - 1)
            def _():
                self.copy_up(a0).start()

            for o in range(1, pc.B):
                self.copy_side(a0, o).start()

        @pl.when(pc.a + r < pc.A)
        def _():
            a0 = pc.a + r
            self.arrived(a0 * pc.B + pc.b)

            @pl.when(pc.a > 0)
            def _():
                self.copy_down(a0).start()

            for o in range(1, pc.B):
                self.copy_side(a0, o).start()

    def rounds(self):
        for r in range(1, self.pc.A):
            self.round(r)

    def pair_arrived(self, a0):
        for o in range(1, self.pc.B):
            self.arrived(a0 * self.pc.B + self.pc.across(o))

    def finish(self):
        pc = self.pc
        for a0 in range(pc.A):
            for o in range(1, pc.B):
                self.copy_side(a0, o).wait_send()

            @pl.when((pc.a >= a0) & (pc.a < pc.A - 1))
            def _():
                self.copy_up(a0).wait_send()

            @pl.when((pc.a <= a0) & (pc.a > 0))
            def _():
                self.copy_down(a0).wait_send()


def gather_sems(n):
    A, B = plane(n)
    dma = pltpu.SemaphoreType.DMA
    return [dma((n,)), dma((A,)), dma((A,)), dma((A, max(B - 1, 1)))]


class Scatter:
    def __init__(self, place, term, side_in, up_in, down_in, up_out, down_out,
                 side_send, side_recv, up_send, up_recv, down_send, down_recv):
        self.pc, self.term = place, term
        self.side_in, self.up_in, self.down_in = side_in, up_in, down_in
        self.up_out, self.down_out = up_out, down_out
        self.side_send, self.side_recv = side_send, side_recv
        self.up_send, self.up_recv = up_send, up_recv
        self.down_send, self.down_recv = down_send, down_recv
        self.rows = term.shape[1]

    def copy_side(self, a0, o):
        pc = self.pc
        return remote(self.term.at[a0 * pc.B + pc.across(o)], self.side_in.at[a0, o - 1],
                      self.side_send.at[a0, o - 1], self.side_recv.at[a0, o - 1],
                      pc.peer(pc.a, pc.across(o)))

    def copy_up(self, d):
        pc = self.pc
        return remote(self.up_out.at[d], self.up_in.at[d], self.up_send.at[d], self.up_recv.at[d],
                      pc.peer(jnp.minimum(pc.a + 1, pc.A - 1), pc.b))

    def copy_down(self, d):
        pc = self.pc
        return remote(self.down_out.at[d], self.down_in.at[d], self.down_send.at[d], self.down_recv.at[d],
                      pc.peer(jnp.maximum(pc.a - 1, 0), pc.b))

    def start(self, d):
        for o in range(1, self.pc.B):
            self.copy_side(d, o).start()

    def local(self, d, rows):
        pc = self.pc
        total = self.term[d * pc.B + pc.b, rows, :].astype(jnp.float32)
        for o in range(1, pc.B):
            total = total + self.side_in[d, o - 1, rows, :].astype(jnp.float32)
        return total

    def forward(self, d, first, arrived, out, make_copy):
        pc = self.pc
        for o in range(1, pc.B):
            self.copy_side(d, o).wait_recv()

        @pl.when(first)
        def _():
            def body(rows):
                out[d, rows, :] = self.local(d, rows).astype(jnp.bfloat16)

            row_loop(self.rows, body)

        @pl.when(jnp.logical_not(first))
        def _():
            make_copy(d).wait_recv()

            def body(rows):
                out[d, rows, :] = (self.local(d, rows) + arrived[d, rows, :].astype(jnp.float32)).astype(jnp.bfloat16)

            row_loop(self.rows, body)

        make_copy(d).start()

    def pass_on(self, d):
        pc = self.pc

        @pl.when(d > pc.a)
        def _():
            self.forward(d, pc.a == 0, self.up_in, self.up_out, self.copy_up)

        @pl.when(d < pc.a)
        def _():
            self.forward(d, pc.a == pc.A - 1, self.down_in, self.down_out, self.copy_down)

    def run(self, compute, ready=0):
        pc = self.pc
        end = (pc.a == 0) | (pc.a == pc.A - 1)

        def step(k, carry):
            d = pc.far(k)
            if ready:

                @pl.when(k >= ready)
                def _():
                    compute(d)

            else:
                compute(d)
            self.start(d)

            @pl.when((k >= 1) & end)
            def _():
                self.pass_on(pc.far(k - 1))

            return carry

        lax.fori_loop(0, pc.A, step, 0)

        @pl.when(jnp.logical_not(end))
        def _():
            def late(k, carry):
                self.pass_on(pc.far(k))
                return carry

            lax.fori_loop(0, pc.A - 1, late, 0)

    def result(self, use):
        pc = self.pc
        for o in range(1, pc.B):
            self.copy_side(pc.a, o).wait_recv()

        @pl.when(pc.a == 0)
        def _():
            self.copy_down(pc.a).wait_recv()
            row_loop(self.rows, lambda rows: use(
                rows, self.local(pc.a, rows) + self.down_in[pc.a, rows, :].astype(jnp.float32)))

        @pl.when(pc.a == pc.A - 1)
        def _():
            self.copy_up(pc.a).wait_recv()
            row_loop(self.rows, lambda rows: use(
                rows, self.local(pc.a, rows) + self.up_in[pc.a, rows, :].astype(jnp.float32)))

        @pl.when((pc.a > 0) & (pc.a < pc.A - 1))
        def _():
            self.copy_up(pc.a).wait_recv()
            self.copy_down(pc.a).wait_recv()
            row_loop(self.rows, lambda rows: use(
                rows, self.local(pc.a, rows) + self.up_in[pc.a, rows, :].astype(jnp.float32)
                + self.down_in[pc.a, rows, :].astype(jnp.float32)))

    def finish(self):
        pc = self.pc
        for d in range(pc.A):
            for o in range(1, pc.B):
                self.copy_side(d, o).wait_send()

            @pl.when(pc.a < d)
            def _():
                self.copy_up(d).wait_send()

            @pl.when(pc.a > d)
            def _():
                self.copy_down(d).wait_send()


def scatter_scratch(n, rows, width):
    A, B = plane(n)
    dma = pltpu.SemaphoreType.DMA
    side = max(B - 1, 1)
    buf = pltpu.VMEM((A, rows, width), jnp.bfloat16)
    return [pltpu.VMEM((A, side, rows, width), jnp.bfloat16), buf, buf, buf, buf,
            dma((A, side)), dma((A, side)), dma((A,)), dma((A,)), dma((A,)), dma((A,))]


def layer_kernel(n, ndp, heads, q_scale, hidden, gain1, gain2, prefix, owners, w_query, w_keyval, seg, w_out,
                 w_fc_hbm, w_proj_hbm, attended, layer_out, *scratch):
    pc = Place(n)
    dp = lax.axis_index("dp")
    w_fc, w_proj, fc_sem, proj_sem, term, normed, normed2, middle, act, projected, cached = scratch[:11]
    from_dp, dp_send, dp_recv = scratch[11:14]
    greet(pc, ndp)
    rows, width = hidden.shape
    slab = pc.B * rows
    row_len = projected.shape[0]
    query_cols = w_query.shape[1]
    head = query_cols // heads
    span = pc.B * cached.shape[1]

    def to_dp(o):
        return remote(prefix.at[0], from_dp.at[dp], dp_send.at[o - 1], dp_recv.at[dp],
                      {"dp": (dp + o) % ndp})

    gains = gain1[...].astype(jnp.float32).reshape(1, width)

    def first(part):
        normed[pc.me, part, :] = norm_rows(hidden[part, :].astype(jnp.float32), gains)

    row_loop(rows, first)
    tokens = Gather(pc, normed, *scratch[14:18])
    tokens.start()
    for o in range(1, ndp):
        to_dp(o).start()
    load_fc = pltpu.make_async_copy(w_fc_hbm, w_fc, fc_sem)
    load_proj = pltpu.make_async_copy(w_proj_hbm, w_proj, proj_sem)
    load_fc.start()
    load_proj.start()
    from_dp[dp] = prefix[0]

    def project(d):
        tokens.pair_arrived(d)
        left = normed[pl.ds(d * pc.B, pc.B)].reshape(slab, width)
        here = pl.ds(pl.multiple_of(d * slab, slab), slab)
        projected[here, :query_cols] = (
            jnp.dot(left, w_query[...], preferred_element_type=jnp.float32) * q_scale
        ).astype(jnp.bfloat16)
        projected[here, query_cols:] = jnp.dot(
            left, w_keyval[...], preferred_element_type=jnp.float32
        ).astype(jnp.bfloat16)

    for r in range(1, pc.A):
        tokens.round(r)
        if r < pc.A - 1:
            project(pc.far(pc.A - r))
    for o in range(1, ndp):
        src = (dp + o) % ndp
        remote(prefix.at[0], from_dp.at[src], dp_send.at[0], dp_recv.at[src],
               {"dp": (dp + 1) % ndp}).wait_recv()
    cached[pc.me] = from_dp[owners[dp]]
    keys = Gather(pc, cached, *scratch[18:22])
    keys.start()
    project(pc.far(1))
    keys.round(1)
    project(pc.far(0))

    def block(q, state, keys_here, values, allowed):
        top, total, weighted = state
        scores = lax.dot_general(q, keys_here, (((1,), (1,)), ((), ())), preferred_element_type=jnp.float32)
        if allowed is not None:
            scores = jnp.where(allowed[None], scores.reshape(heads, slab, -1), -jnp.inf)
            scores = scores.reshape(heads * slab, -1)
        new_top = jnp.maximum(top, jnp.max(scores, axis=-1, keepdims=True))
        factor = jnp.exp(top - new_top)
        probs = jnp.exp(scores - new_top)
        total = total * factor + jnp.sum(probs, axis=-1, keepdims=True)
        weighted = weighted * factor + jnp.dot(
            probs.astype(jnp.bfloat16), values, preferred_element_type=jnp.float32
        )
        return new_top, total, weighted

    def emit(left, weights, d):
        wide = min(512, width)

        def column(c, carry):
            here = pl.ds(pl.multiple_of(c * wide, wide), wide)
            out = jnp.dot(left, weights[:, here], preferred_element_type=jnp.float32)
            term[pl.ds(d * pc.B, pc.B), :, here] = out.astype(jnp.bfloat16).reshape(pc.B, rows, wide)
            return carry

        lax.fori_loop(0, width // wide, column, 0)

    def stacked(d):
        here = pl.ds(pl.multiple_of(d * slab, slab), slab)
        return jnp.concatenate([projected[here, h * head : (h + 1) * head] for h in range(heads)], axis=0)

    def over_suffix(d, q):
        state = (
            jnp.full((heads * slab, 1), -jnp.inf, jnp.float32),
            jnp.zeros((heads * slab, 1), jnp.float32),
            jnp.zeros((heads * slab, head), jnp.float32),
        )
        spot = d * slab + lax.broadcasted_iota(jnp.int32, (slab, row_len), 0)
        other = lax.broadcasted_iota(jnp.int32, (slab, row_len), 1)
        ids = seg[...].astype(jnp.float32)
        mine = jnp.sum(jnp.where(other == spot, ids, 0.0), axis=1, keepdims=True)
        allowed = (other <= spot) & (mine == ids)
        return block(q, state, projected[:, query_cols : query_cols + head],
                     projected[:, query_cols + head :], allowed)

    def over_prefix(e, q, state):
        pair = cached[pl.ds(e * pc.B, pc.B)].reshape(span, 2 * head)
        return block(q, state, pair[:, :head], pair[:, head:], None)

    def heads_done(d, state):
        _, total, weighted = state
        out = (weighted / total).astype(jnp.bfloat16)
        left = jnp.concatenate([out[h * slab : (h + 1) * slab] for h in range(heads)], axis=1)
        emit(left, w_out, d)

    lead = pc.far(0)
    q_lead = stacked(lead)
    state = over_suffix(lead, q_lead)
    for r in range(1, pc.A + 1):
        e = pc.far(pc.A - r)
        keys.pair_arrived(e)
        state = over_prefix(e, q_lead, state)
        if r + 1 < pc.A:
            keys.round(r + 1)
    heads_done(lead, state)

    def attend(d):
        q = stacked(d)
        state = over_suffix(d, q)
        state = lax.fori_loop(0, pc.A, lambda e, state: over_prefix(e, q, state), state)
        heads_done(d, state)

    scatter = Scatter(pc, term, *scratch[26:37])
    scatter.run(attend, ready=1)
    gains2 = gain2[...].astype(jnp.float32).reshape(1, width)

    def use(part, total):
        out = total.astype(jnp.bfloat16)
        attended[part, :] = out
        mid = (hidden[part, :].astype(jnp.float32) + out.astype(jnp.float32)).astype(jnp.bfloat16)
        middle[part, :] = mid
        normed2[pc.me, part, :] = norm_rows(mid.astype(jnp.float32), gains2)

    scatter.result(use)
    gather = Gather(pc, normed2, *scratch[22:26])
    gather.start()
    scatter.finish()
    load_fc.wait()
    load_proj.wait()
    units = w_fc.shape[1]
    wide = min(256, units)

    def expand(d):
        gather.pair_arrived(d)
        here = pl.ds(pl.multiple_of(d * slab, slab), slab)

        def column(c, carry):
            cols = pl.ds(pl.multiple_of(c * wide, wide), wide)
            left = normed2[pl.ds(d * pc.B, pc.B)].reshape(slab, width)
            out = jnp.dot(left, w_fc[:, cols], preferred_element_type=jnp.float32)
            act[here, cols] = jax.nn.gelu(out, approximate=True).astype(jnp.bfloat16)
            return carry

        lax.fori_loop(0, units // wide, column, 0)

    for r in range(1, pc.A):
        gather.round(r)
        expand(pc.far(pc.A - r))
    expand(pc.far(0))

    def contract(d):
        here = pl.ds(pl.multiple_of(d * slab, slab), slab)
        emit(act[here, :], w_proj, d)

    scatter2 = Scatter(pc, term, *scratch[37:])
    scatter2.run(contract)

    def last(part, total):
        layer_out[part, :] = (middle[part, :].astype(jnp.float32) + total).astype(jnp.bfloat16)

    scatter2.result(last)
    tokens.finish()
    keys.finish()
    for o in range(1, ndp):
        to_dp(o).wait_send()
    gather.finish()
    scatter2.finish()


def hand_on(attended, layer_out, attended_to, layer_to):
    attended_to[...] = attended[...]
    layer_to[...] = layer_out[...]


VM = pl.BlockSpec(memory_space=pltpu.VMEM)


def params(cid):
    return pltpu.CompilerParams(collective_id=cid, has_side_effects=True, vmem_limit_bytes=60 << 20)


def local(n, ndp, hidden_in, norm1_gain, norm2_gain, w_query, w_keyval, w_out, w_fc, w_proj,
          prefix_kv, owner_ids, segment_ids):
    rows, width = hidden_in.shape
    head_size = w_keyval.shape[1] // 2
    query_cols = w_query.shape[1]
    heads_here = query_cols // head_size
    row_len = segment_ids.shape[1]
    span = prefix_kv.shape[1]
    q_scale = 1.0 / math.sqrt(head_size)
    bf = jnp.bfloat16
    dma = pltpu.SemaphoreType.DMA
    any_space = pl.BlockSpec(memory_space=pl.ANY)
    own = jax.ShapeDtypeStruct((rows, width), bf)
    shards = pltpu.VMEM((n, rows, width), bf)
    attended, layer_out = pl.pallas_call(
        functools.partial(layer_kernel, n, ndp, heads_here, q_scale),
        out_shape=(own, own),
        in_specs=[VM] * 4 + [pl.BlockSpec(memory_space=pltpu.SMEM)] + [VM] * 4 + [any_space] * 2,
        out_specs=(VM, VM),
        scratch_shapes=[pltpu.VMEM(w_fc.shape, bf), pltpu.VMEM(w_proj.shape, bf), dma(()), dma(()),
                        shards, shards, shards, pltpu.VMEM((rows, width), bf),
                        pltpu.VMEM((row_len, w_fc.shape[1]), bf),
                        pltpu.VMEM((row_len, query_cols + 2 * head_size), bf),
                        pltpu.VMEM((n, span, 2 * head_size), bf),
                        pltpu.VMEM((ndp, span, 2 * head_size), bf), dma((ndp,)), dma((ndp,))]
        + gather_sems(n) * 3 + scatter_scratch(n, rows, width) * 2,
        compiler_params=params(1),
        name="layer",
    )(hidden_in, norm1_gain, norm2_gain, prefix_kv, owner_ids, w_query, w_keyval, segment_ids, w_out,
      w_fc, w_proj)
    attended, layer_out = pl.pallas_call(
        hand_on, out_shape=(own, own), in_specs=[VM] * 2, out_specs=(VM, VM), name="hand_on",
    )(attended, layer_out)
    return (layer_out, attended)


def solution(mesh):
    return jax.shard_map(
        functools.partial(local, mesh.shape["tensor"], mesh.shape["dp"]),
        mesh=mesh,
        in_specs=(
            P(("dp", "tensor"), None),
            P(),
            P(),
            P(None, "tensor"),
            P(),
            P("tensor", None),
            P(None, "tensor"),
            P("tensor", None),
            P("dp", "tensor", None),
            P(),
            P("dp", None),
        ),
        out_specs=(P(("dp", "tensor"), None), P(("dp", "tensor"), None)),
        check_vma=False,
    )
```
